128 devices in a mesh: bx: 16 (over x, y), by: 8 (over z, core).
Axes of the slice: x: 4, y: 4, z: 4, core: 2. Of those that a mesh axis runs over, the one named last changes fastest.
Arguments:
- particle_values: float32 [3, 262144], P(None, ('bx', 'by')), may hold values from -6 to 6
- destination: int32 [262144, 1], P(('bx', 'by')), may hold values from 0 to 127; in each aligned block of 2048 rows (0 to 2047, 2048 to 4095, ...) at most 32 rows name the same one
- cell_index: int32 [262144], P(('bx', 'by')), may hold values from 0 to 16383
- weight_in: bfloat16 [3, 3, 64, 9], replicated, may hold values from -0.625 to 0.625
- weight_mid: bfloat16 [3, 3, 64, 192], replicated, may hold values from -0.15625 to 0.15625
- weight_out: bfloat16 [3, 3, 64, 192], replicated, may hold values from -0.15625 to 0.15625
Outputs:
- spectrum: bfloat16 [2, 64, 16, 128, 1024], P(None, None, 'bx', None, 'by')
The draws below stay inside these ranges and needn't reach their ends.
Inputs may be any that keep to these rules, and one draw needn't show every extreme that they name: `destination`: among the 2048 rows of one device, no brick is named more than 32 times; some brick is named exactly 32 times.
All inputs are finite; a program needn't handle non-finite values.
Results may differ from the reference program's by a relative error of at most 0.0074.
Values may be sent and summed in bfloat16 or wider, within the bound.
No kernel may reach another device: no remote copies, remote signals or barrier semaphores. Data moves between devices by JAX's collectives and lax.ppermute only.
A program may use at most 192 MiB of HBM per device.

```python
import math
import jax
import jax.numpy as jnp
import numpy as np
from jax import lax

C = 64
F_IN = 3
CELL_X = 8
CELL_Y = 128
P_DEV = 2048
CAP = 32
CELLS = 16384
TOTAL_P = 262144
NX = 128
NY = 1024
NZ = 16
N_BY = 8
DEVICES = 128


def touch_ends(array, rng, low, largest):
    longest = array.shape.index(max(array.shape))
    spots = []
    for shift in (0, 1):
        where = [jax.random.randint(jax.random.fold_in(rng, axis), (), 0, length) for axis, length in enumerate(array.shape)]
        where[longest] = (where[longest] + shift) % array.shape[longest]
        spots.append(tuple(where))
    return array.at[spots[0]].set(low).at[spots[1]].set(largest)


def levels(own_key, extent, cuts, smallest, top_value):
    level, own = 1.0, jax.random.fold_in(own_key, 6)
    for dim, shards_of in cuts:
        heights = jnp.exp(jax.random.uniform(jax.random.fold_in(own, dim), (shards_of,), jnp.float32, smallest / len(cuts), top_value / len(cuts)))
        level = level * jnp.repeat(heights, extent[dim] // shards_of).reshape([-1 if axis == dim else 1 for axis in range(len(extent))])
    return level


def deal_out(own_key, own, number, rows, count, top, most, slope):
    ranking = jax.random.permutation(own_key, count)
    heavy_load, ordinary = portions_of(count, rows * top, most, slope, True), portions_of(count, rows * top, most, slope, False)
    places = jnp.arange(count)

    def named(lengths, offset_by):
        used = int((lengths > 0).sum())
        fixed = max(1, used // 4)
        passed = fixed + (places - fixed + offset_by * (used - fixed)) % max(1, count - fixed)
        return jnp.zeros((count,), jnp.int32).at[ranking[jnp.where(places < fixed, places, passed)]].set(jnp.asarray(lengths, jnp.int32))

    lengths = jnp.where(number % 4 == 0, named(heavy_load, number // 4), named(ordinary, number - number // 4 - 1))
    mixed = jax.random.permutation(jax.random.fold_in(own, 3), count)
    giver, taker = mixed[0:count // 2 * 2:2], mixed[1:count // 2 * 2:2]
    margin = jnp.minimum(lengths[giver] - 1, most - lengths[taker]) // 2
    margin = jnp.where((giver == ranking[0]) | (taker == ranking[0]) | (lengths[taker] == 0), 0, jnp.maximum(margin, 0))
    passed = jax.random.randint(jax.random.fold_in(own, 4), (count // 2,), 0, 1 << 20) % (margin + 1)
    lengths = lengths.at[giver].add(-passed).at[taker].add(passed)
    members = jnp.searchsorted(jnp.cumsum(lengths), jnp.arange(rows * top), side="right").astype(jnp.int32)
    grid = members.reshape(top, rows).T
    grid = grid[jax.random.permutation(jax.random.fold_in(own, 1), rows)]
    offset_by = jax.random.randint(jax.random.fold_in(own, 2), (rows, 1), 0, top)
    return jnp.take_along_axis(grid, (jnp.arange(top)[None, :] + offset_by) % top, axis=1)


def portions_of(number_of, total, limit, slope, full):
    weights = [(1 << 20) // math.isqrt(rank ** slope) + 1 for rank in range(1, number_of + 1)]
    largest = limit if full else min(limit, max(-(-total // number_of), total * weights[0] // sum(weights)))
    least = 1 if total - largest >= number_of - 1 else 0
    given, rest = [largest] + [least] * (number_of - 1), total - largest - least * (number_of - 1)
    while rest > 0:
        movable = [i for i in range(1, number_of) if given[i] < largest] or [i for i in range(1, number_of) if given[i] < limit]
        pool, remaining = sum([weights[i] for i in movable]), rest
        for i in movable:
            extra = min(limit - given[i], max(1, remaining * weights[i] // pool), rest)
            given[i] = given[i] + extra
            rest = rest - extra
    return np.array(given)


def centred(rng, dims, scale, most, split=(), kind=jnp.bfloat16):
    factor_of = levels(rng, dims, split, -0.22, 0.18) if split else 1.0
    drawn = jax.random.normal(rng, dims, jnp.float32) * scale * factor_of
    return jnp.minimum(jnp.maximum(drawn, -most), most).astype(kind)


def setup_inputs(seed: int = 0) -> dict:
    key_of = jax.random.split(jax.random.key(seed), 7)
    particle_values = centred(key_of[0], (F_IN, TOTAL_P), 1.0, 6.0, ((1, 128),), jnp.float32)
    destination_keys = jax.random.split(jax.random.fold_in(key_of[1], 1), TOTAL_P // P_DEV)
    destination_turns = jax.random.permutation(jax.random.fold_in(key_of[1], 3), TOTAL_P // P_DEV)
    destination = jax.vmap(lambda own, number: deal_out(jax.random.fold_in(key_of[1], 2), own, number, P_DEV, DEVICES, 1, CAP, 2))(destination_keys, destination_turns).reshape((TOTAL_P, 1))
    cell_index = touch_ends(jax.random.randint(key_of[2], (TOTAL_P,), 0, CELLS), jax.random.fold_in(key_of[2], 1), 0, CELLS - 1).astype(jnp.int32)
    weight_in = centred(key_of[3], (3, 3, C, 3 * F_IN), (27 * F_IN) ** -0.5, 0.625)
    weight_mid = centred(key_of[4], (3, 3, C, 3 * C), (27 * C) ** -0.5, 0.15625)
    weight_out = centred(key_of[5], (3, 3, C, 3 * C), (27 * C) ** -0.5, 0.15625)
    return {"particle_values": particle_values, "destination": destination, "cell_index": cell_index, "weight_in": weight_in, "weight_mid": weight_mid, "weight_out": weight_out}


def convolve(field, weight, spacing):
    channels = field.shape[0]
    depth = field.shape[1]

    def one_plane(plane_z):
        summed = jnp.zeros((weight.shape[2], NX * NY), jnp.float32)
        for step_z in range(3):
            source_z = ((plane_z + (step_z - 1) * spacing) % depth).astype(jnp.int32)
            plane = lax.dynamic_index_in_dim(field, source_z, axis=1, keepdims=False)
            for step_x in range(3):
                for step_y in range(3):
                    shifted = jnp.roll(plane, (-(step_x - 1) * spacing, -(step_y - 1) * spacing), axis=(1, 2))
                    matrix = weight[step_x, step_y][:, step_z * channels:(step_z + 1) * channels]
                    summed = summed + jnp.dot(matrix, shifted.reshape(channels, NX * NY), preferred_element_type=jnp.float32)
        summed = summed.reshape(weight.shape[2], NX, NY)
        return jnp.where(summed > 0, summed, 0.1 * summed).astype(jnp.bfloat16)
    planes = lax.map(one_plane, jnp.arange(depth, dtype=jnp.int32))
    return jnp.transpose(planes, (1, 0, 2, 3))

def twiddle_table(count):
    position = jnp.arange(count, dtype=jnp.int32)
    phase = position[:, None] * position[None, :] % count
    angle = phase.astype(jnp.float32) * (2.0 * math.pi / count)
    factor = 1.0 / math.sqrt(count)
    return jnp.stack([jnp.cos(angle) * factor, -jnp.sin(angle) * factor]).astype(jnp.bfloat16)

def reference(particle_values, destination, cell_index, weight_in, weight_mid, weight_out):
    target = destination[:, 0]
    brick_x = target // N_BY
    brick_y = target % N_BY
    plane = cell_index // (CELL_X * CELL_Y)
    local_x = cell_index // CELL_Y % CELL_X
    local_y = cell_index % CELL_Y
    flat = (plane * NX + brick_x * CELL_X + local_x) * NY + brick_y * CELL_Y + local_y
    painted = jnp.zeros((F_IN, NZ * NX * NY), jnp.float32).at[:, flat].add(particle_values)
    painted = painted.reshape(F_IN, NZ, NX, NY).astype(jnp.bfloat16)
    first = convolve(painted, weight_in, 1)
    second = convolve(first, weight_mid, 2)
    third = convolve(second, weight_out, 1)
    twiddle = twiddle_table(NX).astype(jnp.float32)

    def per_channel(channel_field):
        result = jnp.einsum('tkx,zxy->tzky', twiddle, channel_field.astype(jnp.float32))
        return result.astype(jnp.bfloat16)
    spectrum = lax.map(per_channel, third)
    return jnp.transpose(spectrum, (1, 0, 2, 3, 4))
```

```python
import math

import jax
import jax.numpy as jnp
import numpy as np
from jax import lax
from jax.experimental import pallas as pl
from jax.experimental.pallas import tpu as pltpu
from jax.sharding import PartitionSpec as P

F32 = jnp.float32
BF16 = jnp.bfloat16
I32 = jnp.int32
VMEM = pltpu.VMEM

NT = (((1,), (1,)), ((), ()))
NN = (((1,), (0,)), ((), ()))

Y1 = 144
K_TAPS = 9 * 384


def dot(a, b, dims=NN):
    return lax.dot_general(a, b, dims, preferred_element_type=F32)


def leaky(u):
    return jnp.where(u > 0, u, 0.1 * u)


def split2(v):
    high = v.astype(BF16)
    return high, (v - high.astype(F32)).astype(BF16)


def pack_kernel(dest_ref, cell_ref, value_ref, out_ref):
    rows = dest_ref.shape[1]
    step = 256
    brick = lax.broadcasted_iota(I32, (128, step), 0)
    before = (
        lax.broadcasted_iota(I32, (step, step), 0) < lax.broadcasted_iota(I32, (step, step), 1)
    ).astype(F32).astype(BF16)
    slot_ids = lax.broadcasted_iota(I32, (32, step), 0)
    seen = jnp.zeros((128, 1), F32)
    total = jnp.zeros((128, 256), F32)
    for start in range(0, rows, step):
        here = slice(start, start + step)
        hot = (brick == dest_ref[:, here]).astype(F32)
        hot_b = hot.astype(BF16)
        prefix = dot(hot_b, before) + seen
        slot = jnp.sum(hot * prefix, axis=0, keepdims=True).astype(I32)
        seen = prefix[:, step - 1 :] + hot[:, step - 1 :]
        mine = slot_ids == slot
        pieces = [cell_ref[:, here].astype(F32)] + [value_ref[f : f + 1, here] for f in range(3)]
        highs, lows = [], []
        for piece in pieces:
            high = piece.astype(BF16).astype(F32)
            highs.append(jnp.where(mine, high, 0.0))
            lows.append(jnp.where(mine, piece - high, 0.0))
        spread = jnp.concatenate(highs + lows, axis=0).astype(BF16)
        total = total + dot(hot_b, spread, NT)
    out_ref[...] = total[:, :128] + total[:, 128:]


def pack(dest, cell, values):
    return pl.pallas_call(
        pack_kernel,
        out_shape=jax.ShapeDtypeStruct((128, 128), F32),
        name="pack",
    )(dest, cell, values)


def paint_kernel(in_ref, left_ref, right_ref, acc_ref):
    turned = jnp.transpose(in_ref[...], (1, 0))
    cells = turned[0:32].astype(I32)
    place = ((cells >> 8) & 3) * 128 + (cells & 127)
    parity = (cells >> 7) & 1
    depth = cells >> 10
    code = parity * 16 + depth
    parts = []
    for f in range(3):
        value = turned[32 + 32 * f : 64 + 32 * f]
        high = value.astype(BF16).astype(F32)
        parts.append((high, value - high))
    z_ids = lax.broadcasted_iota(I32, (16, 128), 0)
    place_ids = lax.broadcasted_iota(I32, (512, 128), 0)
    blank = jnp.zeros((16, 128), F32)
    group = 8
    for start in range(0, 32, group):
        hots, sides = [], []
        for s in range(start, start + group):
            hots.append((place_ids == place[s : s + 1]).astype(F32).astype(BF16))
            column = []
            for part in range(2):
                for par in range(2):
                    here = z_ids + par * 16 == code[s : s + 1]
                    for f in range(3):
                        column.append(jnp.where(here, parts[f][part][s : s + 1], 0.0))
                    column.append(blank)
            sides.append(jnp.concatenate(column, axis=0).astype(BF16))
        added = dot(jnp.concatenate(hots, axis=1), jnp.concatenate(sides, axis=1), NT)
        if start == 0:
            acc_ref[...] = added
        else:
            acc_ref[...] += added
    painted = (acc_ref[:, :128] + acc_ref[:, 128:]).astype(BF16)
    left_ref[...] = painted[:256].reshape(2, 128, 128)
    right_ref[...] = painted[256:].reshape(2, 128, 128)


def paint(incoming):
    half = jax.ShapeDtypeStruct((2, 128, 128), BF16)
    return pl.pallas_call(
        paint_kernel,
        out_shape=(half, half),
        scratch_shapes=[VMEM((512, 256), F32)],
        name="paint",
    )(incoming)


def weights_kernel(win_ref, wmid_ref, wout_ref, r1_ref, r2_ref, w3_ref):
    lane = lax.broadcasted_iota(I32, (16, 1024), 1)
    tile = lane // 128
    half = (lane // 64) % 2
    z_out = jnp.where(tile < 4, 14 + 4 * tile + 2 * half, 13 + 4 * (tile - 4) + 2 * half) % 16
    tap_z = (lax.broadcasted_iota(I32, (16, 1024), 0) - z_out + 17) % 16
    hits = [tap_z == tz for tz in range(3)]
    blank = jnp.zeros((64, 1024), BF16)
    for ty in range(3):
        for tx in range(3):
            column = []
            for f in range(3):
                block = jnp.zeros((16, 1024), F32)
                for tz in range(3):
                    row = ((tx * 3 + ty) * 3 + tz) * 3 + f
                    block = jnp.where(hits[tz], win_ref[row : row + 1, :], block)
                column.append(block)
            column.append(jnp.zeros((16, 1024), F32))
            block = jnp.concatenate(column, axis=0).astype(BF16)
            for out in range(2):
                at = ty * 256 + (tx + out) * 64
                r1_ref[at : at + 64, out * 1024 : out * 1024 + 1024] = block
        r1_ref[ty * 256 + 192 : ty * 256 + 256, 0:1024] = blank
        r1_ref[ty * 256 : ty * 256 + 64, 1024:2048] = blank
    low = lax.broadcasted_iota(I32, (384, 128), 1) < 64
    for tap in range(9):
        turned = wmid_ref[tap].astype(F32)
        shifted = []
        for j in range(4):
            pieces = [turned]
            if j:
                pieces = [jnp.zeros((64 * j, 128), F32)] + pieces
            if j < 3:
                pieces = pieces + [jnp.zeros((192 - 64 * j, 128), F32)]
            shifted.append(jnp.concatenate(pieces, axis=0))
        for h in range(2):
            a, b = shifted[2 * h], shifted[2 * h + 1]
            rows = slice(tap * 384, tap * 384 + 384)
            r2_ref[0, rows, h * 128 : h * 128 + 128] = jnp.where(low, b, a).astype(BF16)
            r2_ref[1, rows, h * 128 : h * 128 + 128] = jnp.where(low, a, b).astype(BF16)
    low = lax.broadcasted_iota(I32, (64, 128), 1) < 64
    none = jnp.zeros((64, 128), BF16)
    for tap in range(9):
        w01 = wout_ref[tap, :, 0:128].astype(F32)
        w2_ = wout_ref[tap, :, 128:256].astype(F32)
        w10 = pltpu.roll(w01, 64, axis=1)
        w_2 = pltpu.roll(w2_, 64, axis=1)
        zero = jnp.zeros((64, 128), F32)
        table = [
            [w01, w_2, None],
            [jnp.where(low, zero, w10), jnp.where(low, w2_, w01), None],
            [None, w10, w2_],
            [None, jnp.where(low, w01, zero), jnp.where(low, w10, w_2)],
        ]
        for j in range(4):
            for t in range(3):
                at = tap * 384 + t * 128
                piece = table[j][t]
                w3_ref[64 * j : 64 * j + 64, at : at + 128] = none if piece is None else piece.astype(BF16)


def weights(win, wmid, wout):
    return pl.pallas_call(
        weights_kernel,
        out_shape=(
            jax.ShapeDtypeStruct((768, 2048), BF16),
            jax.ShapeDtypeStruct((2, K_TAPS, 256), BF16),
            jax.ShapeDtypeStruct((256, K_TAPS), BF16),
        ),
        name="weights",
    )(win, wmid, wout)


def layers_kernel(
    left_ref, right_ref, xl_ref, xr_ref, top_ref, bottom_ref, r1_ref, r2_ref, w3_ref,
    out_ref, ext_ref, v1_ref, tmp_ref, first_ref, second_ref, third_ref,
):
    ext_ref[:, 144:160] = jnp.zeros((8, 16, 128), F32)
    ext_ref[:, 0:8] = top_ref[...].astype(F32)
    ext_ref[:, 136:144] = bottom_ref[...].astype(F32)
    for at, source in enumerate((xl_ref, left_ref, right_ref, xr_ref)):
        ext_ref[2 * at : 2 * at + 2, 8:136] = source[...].astype(F32)
    for ty in range(3):
        for pair in range(8):
            v1_ref[ty, pair * Y1 : pair * Y1 + Y1] = ext_ref[pair, 4 + ty : 4 + ty + Y1].astype(BF16)
    tmp_ref[:, :, Y1:152] = jnp.zeros((2, 7, 8, 128), F32)

    def first_columns(column, carry):
        lhs = jnp.concatenate(
            [v1_ref[ty, p * Y1 : p * Y1 + 7 * Y1] for ty in range(3) for p in range(2)], axis=1
        )
        at = pl.multiple_of(column * 256, 256)
        u = leaky(dot(lhs, r1_ref[:, pl.ds(at, 256)]))
        for h in range(2):
            tmp_ref[h, :, 0:Y1] = u[:, h * 128 : h * 128 + 128].reshape(7, Y1, 128)
        out = column // 4
        for h in range(2):
            tile = (column % 4) * 2 + h
            for m in range(7):
                row = pl.multiple_of((2 * m + out) * Y1, Y1)
                for s in range(3):
                    first_ref[s, tile, pl.ds(row, Y1)] = tmp_ref[h, m, 2 * s : 2 * s + Y1].astype(BF16)
        return carry

    lax.fori_loop(0, 8, first_columns, 0)

    low = lax.broadcasted_iota(I32, (5 * Y1, 128), 1) < 64

    def second_rows(step, carry):
        group = step // 2
        b = step % 2
        outs = []
        for parity in range(2):
            pieces = []
            for tx in range(3):
                row = pl.multiple_of((group * 5 + 2 * tx) * Y1, Y1)
                for ty in range(3):
                    for w in range(3):
                        tile = parity * 4 + (2 * b + w) % 4
                        pieces.append(first_ref[ty, tile, pl.ds(row, 5 * Y1)])
            outs.append(leaky(dot(jnp.concatenate(pieces, axis=1), r2_ref[parity])))
        even, odd = outs
        for h in range(2):
            e = even[:, h * 128 : h * 128 + 128]
            o = odd[:, h * 128 : h * 128 + 128]
            for k, merged in enumerate((jnp.where(low, o, e), jnp.where(low, e, o))):
                tmp_ref[k, 0:5, 0:Y1] = merged.reshape(5, Y1, 128)
            for k in range(2):
                tile = 4 * b + 2 * h + k
                for q in range(5):
                    row = pl.multiple_of((group * 5 + q) * 128, 128)
                    for s in range(3):
                        second_ref[s, tile, pl.ds(row, 128)] = tmp_ref[k, q, s : s + 128].astype(BF16)
        return carry

    lax.fori_loop(0, 4, second_rows, 0)

    def third_planes(b, carry):
        for pair in range(4):
            pieces = []
            for tx in range(3):
                row = (2 * pair + tx) * 128
                for ty in range(3):
                    for w in range(3):
                        tile = (2 * b + w) % 8
                        pieces.append(second_ref[ty, tile, row : row + 256])
            u = leaky(dot(w3_ref[...], jnp.concatenate(pieces, axis=1), NT))
            for j in range(4):
                for k in range(2):
                    third_ref[j, pl.ds(2 * pair + k, 64, stride=8), :] = (
                        u[64 * j : 64 * j + 64, k * 128 : k * 128 + 128]
                    )
        for j in range(4):
            out_ref[4 * b + j] = third_ref[j].astype(BF16)
        return carry

    lax.fori_loop(0, 4, third_planes, 0)


def layers(left, right, xl, xr, top, bottom, r1, r2, w3):
    return pl.pallas_call(
        layers_kernel,
        out_shape=jax.ShapeDtypeStruct((16, 512, 128), BF16),
        scratch_shapes=[
            VMEM((8, 160, 128), F32),
            VMEM((3, 8 * Y1, 128), BF16),
            VMEM((2, 7, 152, 128), F32),
            VMEM((3, 8, 14 * Y1, 128), BF16),
            VMEM((3, 8, 10 * 128, 128), BF16),
            VMEM((4, 512, 128), F32),
        ],
        compiler_params=pltpu.CompilerParams(vmem_limit_bytes=60 << 20),
        name="layers",
    )(left, right, xl, xr, top, bottom, r1, r2, w3)


def twiddle_rows(count):
    position = np.arange(count, dtype=np.int64)
    phase = position[:, None] * position[None, :] % count
    angle = phase.astype(np.float32) * np.float32(2.0 * math.pi / count)
    factor = np.float32(1.0 / math.sqrt(count))
    parts = np.stack([np.cos(angle) * factor, -np.sin(angle) * factor])
    parts = parts.reshape(2 * count, count // 8, 8)
    table = np.zeros((2, 2 * count, count // 8, 2, 8), np.float32)
    for parity in range(2):
        table[parity, :, :, parity, :] = parts
    return table.reshape(4 * count, 2 * count)


def transform_kernel(twiddle_ref, in_ref, out_ref):
    for pair in range(2):
        rhs = jnp.concatenate(
            [
                in_ref[:, (2 * pair + k) * 16 : (2 * pair + k) * 16 + 16].reshape(256, 128)
                for k in range(2)
            ],
            axis=1,
        )
        u = dot(twiddle_ref[...], rhs).astype(BF16)
        for k in range(2):
            for parity in range(2):
                for t in range(2):
                    at = (parity * 2 + t) * 128
                    out_ref[t, 4 * pair + 2 * k + parity, 0] = u[at : at + 128, k * 128 : k * 128 + 128]


def transform(twiddle, moved):
    return pl.pallas_call(
        transform_kernel,
        grid=(8,),
        in_specs=[
            pl.BlockSpec((512, 256), lambda i: (0, 0)),
            pl.BlockSpec((16, 64, 128), lambda i: (0, i, 0)),
        ],
        out_specs=pl.BlockSpec((2, 8, 1, 128, 128), lambda i: (0, i, 0, 0, 0)),
        out_shape=jax.ShapeDtypeStruct((2, 64, 1, 128, 128), BF16),
        name="transform",
    )(twiddle, moved)


def on_device(particle_values, destination, cell_index, weight_in, weight_mid, weight_out):
    count_x = lax.axis_size("bx")
    count_y = lax.axis_size("by")
    up_x = [(i, (i + 1) % count_x) for i in range(count_x)]
    down_x = [((i + 1) % count_x, i) for i in range(count_x)]
    up_y = [(i, (i + 1) % count_y) for i in range(count_y)]
    down_y = [((i + 1) % count_y, i) for i in range(count_y)]

    outgoing = pack(destination.reshape(1, -1), cell_index.reshape(1, -1), particle_values)
    incoming = lax.all_to_all(outgoing, ("bx", "by"), split_axis=0, concat_axis=0, tiled=True)

    win = jnp.transpose(weight_in.reshape(9, 64, 9), (0, 2, 1)).reshape(81, 64)
    win = jnp.tile(win.astype(F32), (1, 16))
    wmid = jnp.transpose(weight_mid.reshape(9, 64, 192), (0, 2, 1))
    wmid = jnp.concatenate([wmid, wmid], axis=2)
    wout = jnp.pad(weight_out.reshape(9, 64, 192), ((0, 0), (0, 0), (0, 64)))
    r1, r2, w3 = weights(win, wmid, wout)

    left, right = paint(incoming)
    xl = lax.ppermute(right, "bx", up_x)
    xr = lax.ppermute(left, "bx", down_x)
    columns = (xl, left, right, xr)
    top = lax.ppermute(jnp.concatenate([c[:, 120:128] for c in columns], axis=0), "by", up_y)
    bottom = lax.ppermute(jnp.concatenate([c[:, 0:8] for c in columns], axis=0), "by", down_y)

    third = layers(left, right, xl, xr, top, bottom, r1, r2, w3)
    moved = lax.all_to_all(third, "bx", split_axis=0, concat_axis=0, tiled=True)
    twiddle = jnp.asarray(twiddle_rows(count_x * 8), BF16)
    return transform(twiddle, moved)


def solution(mesh):
    placed = (P(None, ("bx", "by")), P(("bx", "by"), None), P(("bx", "by")), P(), P(), P())
    return jax.shard_map(
        on_device,
        mesh=mesh,
        in_specs=placed,
        out_specs=P(None, None, "bx", None, "by"),
        check_vma=False,
    )
```

```python
import math

import jax
import jax.numpy as jnp
import numpy as np
from jax import lax
from jax.experimental import pallas as pl
from jax.experimental.pallas import tpu as pltpu
from jax.sharding import PartitionSpec as P

F32 = jnp.float32
BF16 = jnp.bfloat16
I32 = jnp.int32
VMEM = pltpu.VMEM

NT = (((1,), (1,)), ((), ()))
NN = (((1,), (0,)), ((), ()))

Y1 = 144
K_TAPS = 9 * 384


def dot(a, b, dims=NN):
    return lax.dot_general(a, b, dims, preferred_element_type=F32)


def leaky(u):
    return jnp.where(u > 0, u, 0.1 * u)


def split2(v):
    high = v.astype(BF16)
    return high, (v - high.astype(F32)).astype(BF16)


def pack_kernel(dest_ref, cell_ref, value_ref, out_ref):
    rows = dest_ref.shape[1]
    step = 256
    brick = lax.broadcasted_iota(I32, (128, step), 0)
    before = (
        lax.broadcasted_iota(I32, (step, step), 0) < lax.broadcasted_iota(I32, (step, step), 1)
    ).astype(F32).astype(BF16)
    slot_ids = lax.broadcasted_iota(I32, (32, step), 0)
    seen = jnp.zeros((128, 1), F32)
    total = jnp.zeros((128, 256), F32)
    for start in range(0, rows, step):
        here = slice(start, start + step)
        hot = (brick == dest_ref[:, here]).astype(F32)
        hot_b = hot.astype(BF16)
        prefix = dot(hot_b, before) + seen
        slot = jnp.sum(hot * prefix, axis=0, keepdims=True).astype(I32)
        seen = prefix[:, step - 1 :] + hot[:, step - 1 :]
        mine = slot_ids == slot
        pieces = [cell_ref[:, here].astype(F32)] + [value_ref[f : f + 1, here] for f in range(3)]
        highs, lows = [], []
        for piece in pieces:
            high = piece.astype(BF16).astype(F32)
            highs.append(jnp.where(mine, high, 0.0))
            lows.append(jnp.where(mine, piece - high, 0.0))
        spread = jnp.concatenate(highs + lows, axis=0).astype(BF16)
        total = total + dot(hot_b, spread, NT)
    out_ref[...] = total[:, :128] + total[:, 128:]


def pack(dest, cell, values):
    return pl.pallas_call(
        pack_kernel,
        out_shape=jax.ShapeDtypeStruct((128, 128), F32),
        name="pack",
    )(dest, cell, values)


def paint_kernel(in_any, after_any, left_ref, right_ref, acc_ref, in_ref, sem):
    copy = pltpu.make_async_copy(in_any, in_ref, sem)
    copy.start()
    copy.wait()
    turned = jnp.transpose(in_ref[...], (1, 0))
    cells = turned[0:32].astype(I32)
    place = ((cells >> 8) & 3) * 128 + (cells & 127)
    parity = (cells >> 7) & 1
    depth = cells >> 10
    code = parity * 16 + depth
    parts = []
    for f in range(3):
        value = turned[32 + 32 * f : 64 + 32 * f]
        high = value.astype(BF16).astype(F32)
        parts.append((high, value - high))
    z_ids = lax.broadcasted_iota(I32, (16, 128), 0)
    place_ids = lax.broadcasted_iota(I32, (512, 128), 0)
    blank = jnp.zeros((16, 128), F32)
    group = 8
    for start in range(0, 32, group):
        hots, sides = [], []
        for s in range(start, start + group):
            hots.append((place_ids == place[s : s + 1]).astype(F32).astype(BF16))
            column = []
            for part in range(2):
                for par in range(2):
                    here = z_ids + par * 16 == code[s : s + 1]
                    for f in range(3):
                        column.append(jnp.where(here, parts[f][part][s : s + 1], 0.0))
                    column.append(blank)
            sides.append(jnp.concatenate(column, axis=0).astype(BF16))
        added = dot(jnp.concatenate(hots, axis=1), jnp.concatenate(sides, axis=1), NT)
        if start == 0:
            acc_ref[...] = added
        else:
            acc_ref[...] += added
    painted = (acc_ref[:, :128] + acc_ref[:, 128:]).astype(BF16)
    left_ref[...] = painted[:256].reshape(2, 128, 128)
    right_ref[...] = painted[256:].reshape(2, 128, 128)


def paint(incoming, after):
    half = jax.ShapeDtypeStruct((2, 128, 128), BF16)
    return pl.pallas_call(
        paint_kernel,
        in_specs=[pl.BlockSpec(memory_space=pl.ANY)] * 2,
        out_shape=(half, half),
        scratch_shapes=[VMEM((512, 256), F32), VMEM((128, 128), F32), pltpu.SemaphoreType.DMA(())],
        name="paint",
    )(incoming, after)


def weights_kernel(win_ref, wmid_ref, wout_ref, r1_ref, w2_ref, w3_ref):
    lane = lax.broadcasted_iota(I32, (16, 128), 1)
    depth = lax.broadcasted_iota(I32, (16, 128), 0)
    blank = jnp.zeros((16, 128), F32)
    hits = []
    for tile in range(8):
        first_z = 14 + 4 * tile if tile < 4 else 13 + 4 * (tile - 4)
        tap_z = (depth - first_z - 2 * (lane // 64) + 49) % 16
        hits.append([tap_z == tz for tz in range(3)])
    for tx in range(3):
        for ty in range(3):
            rows = [
                [
                    jnp.broadcast_to(
                        jnp.concatenate([win_ref[tx, tz * 3 + f, ty : ty + 1, :].astype(F32)] * 2, axis=1),
                        (16, 128),
                    )
                    for tz in range(3)
                ]
                for f in range(3)
            ]
            for tile in range(8):
                column = []
                for f in range(3):
                    block = blank
                    for tz in range(3):
                        block = jnp.where(hits[tile][tz], rows[f][tz], block)
                    column.append(block)
                block = jnp.concatenate(column + [blank], axis=0).astype(BF16)
                for out in range(2):
                    at = ty * 256 + (tx + out) * 64
                    r1_ref[out * 8 + tile, at : at + 64] = block
    none = jnp.zeros((64, 128), BF16)
    for ty in range(3):
        for tile in range(8):
            r1_ref[tile, ty * 256 + 192 : ty * 256 + 256] = none
            r1_ref[8 + tile, ty * 256 : ty * 256 + 64] = none
    low = lax.broadcasted_iota(I32, (64, 128), 1) < 64
    zero = jnp.zeros((64, 128), F32)
    for source, target, swap in ((wmid_ref, w2_ref, False), (wout_ref, w3_ref, True)):
        for tap in range(9):
            w01 = source[tap // 3, tap % 3, :, 0:128].astype(F32)
            w2_ = jnp.concatenate(
                [source[tap // 3, tap % 3, :, 128:192].astype(F32), jnp.zeros((64, 64), F32)], axis=1
            )
            w10 = pltpu.roll(w01, 64, axis=1)
            w_2 = pltpu.roll(w2_, 64, axis=1)
            w_0 = jnp.where(low, zero, w10)
            w12 = jnp.where(low, w10, w_2)
            if swap:
                table = [
                    [w01, w_2, None],
                    [w_0, jnp.where(low, w2_, w01), None],
                    [None, w10, w2_],
                    [None, jnp.where(low, w01, zero), w12],
                ]
            else:
                table = [[w01, w2_, None], [w_0, w12, None], [None, w01, w2_], [None, w_0, w12]]
            for j in range(4):
                for t in range(3):
                    piece = table[j][t]
                    target[tap * 3 + t, 64 * j : 64 * j + 64] = none if piece is None else piece.astype(BF16)


def weights(win, wmid, wout):
    return pl.pallas_call(
        weights_kernel,
        out_shape=(
            jax.ShapeDtypeStruct((16, 768, 128), BF16),
            jax.ShapeDtypeStruct((27, 256, 128), BF16),
            jax.ShapeDtypeStruct((27, 256, 128), BF16),
        ),
        name="weights",
    )(win, wmid, wout)


def layers_kernel(
    left_ref, right_ref, xl_any, xr_any, top_any, bottom_any, r1_any, w2_any, w3_any, out_any,
    xl_ref, xr_ref, top_ref, bottom_ref, r1_ref, w2_ref, w3_ref,
    ext_ref, v1_ref, tmp_ref, first_ref, second_ref, rows_ref, third_ref, out_ref, in_sem, out_sem,
):
    pairs = (
        (xl_any, xl_ref), (xr_any, xr_ref), (top_any, top_ref), (bottom_any, bottom_ref),
        (r1_any, r1_ref), (w2_any, w2_ref), (w3_any, w3_ref),
    )
    copies = [pltpu.make_async_copy(a, b, in_sem.at[i]) for i, (a, b) in enumerate(pairs)]
    for copy in copies:
        copy.start()
    ext_ref[:, 144:160] = jnp.zeros((8, 16, 128), F32)
    tmp_ref[:, :, Y1:152] = jnp.zeros((2, 7, 8, 128), F32)
    for copy in copies[:4]:
        copy.wait()
    ext_ref[:, 0:8] = top_ref[...].astype(F32)
    ext_ref[:, 136:144] = bottom_ref[...].astype(F32)
    for at, source in enumerate((xl_ref, left_ref, right_ref, xr_ref)):
        ext_ref[2 * at : 2 * at + 2, 8:136] = source[...].astype(F32)
    for ty in range(3):
        for pair in range(8):
            v1_ref[ty, pair * Y1 : pair * Y1 + Y1] = ext_ref[pair, 4 + ty : 4 + ty + Y1].astype(BF16)
    copies[4].wait()

    def first_columns(column, carry):
        lhs = jnp.concatenate(
            [v1_ref[ty, p * Y1 : p * Y1 + 7 * Y1] for ty in range(3) for p in range(2)], axis=1
        )
        rhs = jnp.concatenate([r1_ref[2 * column], r1_ref[2 * column + 1]], axis=1)
        u = leaky(dot(lhs, rhs))
        for h in range(2):
            tmp_ref[h, :, 0:Y1] = u[:, h * 128 : h * 128 + 128].reshape(7, Y1, 128)
        out = column // 4
        for h in range(2):
            tile = (column % 4) * 2 + h
            for m in range(7):
                row = pl.multiple_of((2 * m + out) * Y1, Y1)
                for s in range(3):
                    first_ref[s, tile, pl.ds(row, Y1)] = tmp_ref[h, m, 2 * s : 2 * s + Y1].astype(BF16)
        return carry

    lax.fori_loop(0, 8, first_columns, 0)
    copies[5].wait()

    low = lax.broadcasted_iota(I32, (5 * Y1, 128), 1) < 64

    def second_rows(step, carry):
        group = step // 2
        b = step % 2
        outs = []
        for parity in range(2):
            pieces = []
            for tx in range(3):
                row = pl.multiple_of((group * 5 + 2 * tx) * Y1, Y1)
                for ty in range(3):
                    for w in range(3):
                        tile = parity * 4 + (2 * b + w) % 4
                        pieces.append(first_ref[ty, tile, pl.ds(row, 5 * Y1)])
            order = (0, 1, 2, 3) if parity else (1, 0, 3, 2)
            rhs = jnp.concatenate(
                [
                    jnp.concatenate([w2_ref[k, 64 * j : 64 * j + 64] for j in order], axis=0)
                    for k in range(27)
                ],
                axis=1,
            )
            outs.append(leaky(dot(jnp.concatenate(pieces, axis=1), rhs, NT)))
        even, odd = outs
        for h in range(2):
            e = even[:, h * 128 : h * 128 + 128]
            o = odd[:, h * 128 : h * 128 + 128]
            for k, merged in enumerate((jnp.where(low, o, e), jnp.where(low, e, o))):
                tmp_ref[k, 0:5, 0:Y1] = merged.reshape(5, Y1, 128)
            for k in range(2):
                tile = 4 * b + 2 * h + k
                for q in range(5):
                    row = pl.multiple_of((group * 5 + q) * 128, 128)
                    for s in range(3):
                        second_ref[s, tile, pl.ds(row, 128)] = tmp_ref[k, q, s : s + 128].astype(BF16)
        return carry

    lax.fori_loop(0, 4, second_rows, 0)
    copies[6].wait()

    def third_rows(b):
        pieces = []
        for tx in range(3):
            for ty in range(3):
                for w in range(3):
                    pieces.append(second_ref[ty, (2 * b + w) % 8, tx * 128 : tx * 128 + 1024])
        rhs = jnp.concatenate([w3_ref[k] for k in range(27)], axis=1)
        u = leaky(dot(jnp.concatenate(pieces, axis=1), rhs, NT))
        for h in range(2):
            rows_ref[b % 2, h] = u[:, h * 128 : h * 128 + 128]

    def third_planes(b):
        for x in range(8):
            for h in range(2):
                turned = jnp.transpose(rows_ref[b % 2, h, x * 128 : x * 128 + 128], (1, 0))
                for k in range(2):
                    third_ref[2 * h + k, pl.ds(x, 64, stride=8), :] = turned[64 * k : 64 * k + 64]
        for j in range(4):
            out_ref[4 * b + j] = third_ref[j].astype(BF16)
        copy = pltpu.make_async_copy(
            out_ref.at[4 * b : 4 * b + 4], out_any.at[4 * b : 4 * b + 4], out_sem.at[b]
        )
        copy.start()
        return copy

    sent = []
    for b in range(4):
        third_rows(b)
        if b:
            sent.append(third_planes(b - 1))
    sent.append(third_planes(3))
    for copy in sent:
        copy.wait()


def layers(left, right, xl, xr, top, bottom, r1, w2, w3):
    whole = pl.BlockSpec(memory_space=pltpu.VMEM)
    anywhere = pl.BlockSpec(memory_space=pl.ANY)
    return pl.pallas_call(
        layers_kernel,
        in_specs=[whole] * 2 + [anywhere] * 7,
        out_specs=anywhere,
        out_shape=jax.ShapeDtypeStruct((16, 512, 128), BF16),
        scratch_shapes=[
            VMEM((2, 128, 128), BF16),
            VMEM((2, 128, 128), BF16),
            VMEM((8, 8, 128), BF16),
            VMEM((8, 8, 128), BF16),
            VMEM((16, 768, 128), BF16),
            VMEM((27, 256, 128), BF16),
            VMEM((27, 256, 128), BF16),
            VMEM((8, 160, 128), F32),
            VMEM((3, 8 * Y1, 128), BF16),
            VMEM((2, 7, 152, 128), F32),
            VMEM((3, 8, 14 * Y1, 128), BF16),
            VMEM((3, 8, 10 * 128, 128), BF16),
            VMEM((2, 2, 1024, 128), F32),
            VMEM((4, 512, 128), F32),
            VMEM((16, 512, 128), BF16),
            pltpu.SemaphoreType.DMA((7,)),
            pltpu.SemaphoreType.DMA((4,)),
        ],
        compiler_params=pltpu.CompilerParams(vmem_limit_bytes=60 << 20),
        name="layers",
    )(left, right, xl, xr, top, bottom, r1, w2, w3)


def twiddle_rows(count):
    position = np.arange(count, dtype=np.int64)
    phase = position[:, None] * position[None, :] % count
    angle = phase.astype(np.float32) * np.float32(2.0 * math.pi / count)
    factor = np.float32(1.0 / math.sqrt(count))
    parts = np.stack([np.cos(angle) * factor, -np.sin(angle) * factor])
    parts = parts.reshape(2 * count, count // 8, 8)
    table = np.zeros((2, 2 * count, count // 8, 2, 8), np.float32)
    for parity in range(2):
        table[parity, :, :, parity, :] = parts
    return table.reshape(4 * count, 2, count).transpose(1, 0, 2)


def transform_kernel(twiddle_ref, in_ref, out_ref):
    lhs = jnp.concatenate([twiddle_ref[0], twiddle_ref[1]], axis=1)
    for pair in range(4):
        rhs = jnp.concatenate(
            [
                in_ref[:, (2 * pair + k) * 16 : (2 * pair + k) * 16 + 16].reshape(256, 128)
                for k in range(2)
            ],
            axis=1,
        )
        u = dot(lhs, rhs).astype(BF16)
        for k in range(2):
            for parity in range(2):
                for t in range(2):
                    at = (parity * 2 + t) * 128
                    out_ref[t, 4 * pair + 2 * k + parity, 0] = u[at : at + 128, k * 128 : k * 128 + 128]


def transform(twiddle, moved):
    return pl.pallas_call(
        transform_kernel,
        grid=(4,),
        in_specs=[
            pl.BlockSpec((2, 512, 128), lambda i: (0, 0, 0)),
            pl.BlockSpec((16, 128, 128), lambda i: (0, i, 0)),
        ],
        out_specs=pl.BlockSpec((2, 16, 1, 128, 128), lambda i: (0, i, 0, 0, 0)),
        out_shape=jax.ShapeDtypeStruct((2, 64, 1, 128, 128), BF16),
        name="transform",
    )(twiddle, moved)


def on_device(particle_values, destination, cell_index, weight_in, weight_mid, weight_out):
    count_x = lax.axis_size("bx")
    count_y = lax.axis_size("by")
    up_x = [(i, (i + 1) % count_x) for i in range(count_x)]
    down_x = [((i + 1) % count_x, i) for i in range(count_x)]
    up_y = [(i, (i + 1) % count_y) for i in range(count_y)]
    down_y = [((i + 1) % count_y, i) for i in range(count_y)]

    outgoing = pack(destination.reshape(1, -1), cell_index.reshape(1, -1), particle_values)
    incoming = lax.all_to_all(outgoing, ("bx", "by"), split_axis=0, concat_axis=0, tiled=True)

    r1, w2, w3 = weights(jnp.transpose(weight_in, (0, 3, 1, 2)), weight_mid, weight_out)

    left, right = paint(incoming, r1)
    xl = lax.ppermute(right, "bx", up_x)
    xr = lax.ppermute(left, "bx", down_x)
    columns = (xl, left, right, xr)
    top = lax.ppermute(jnp.concatenate([c[:, 120:128] for c in columns], axis=0), "by", up_y)
    bottom = lax.ppermute(jnp.concatenate([c[:, 0:8] for c in columns], axis=0), "by", down_y)

    third = layers(left, right, xl, xr, top, bottom, r1, w2, w3)
    moved = lax.all_to_all(third, "bx", split_axis=0, concat_axis=0, tiled=True)
    twiddle = jnp.asarray(twiddle_rows(count_x * 8), BF16)
    return transform(twiddle, moved)


def solution(mesh):
    placed = (P(None, ("bx", "by")), P(("bx", "by"), None), P(("bx", "by")), P(), P(), P())
    return jax.shard_map(
        on_device,
        mesh=mesh,
        in_specs=placed,
        out_specs=P(None, None, "bx", None, "by"),
        check_vma=False,
    )
```

```python
import math

import jax
import jax.numpy as jnp
import numpy as np
from jax import lax
from jax.experimental import pallas as pl
from jax.experimental.pallas import tpu as pltpu
from jax.sharding import PartitionSpec as P

F32 = jnp.float32
BF16 = jnp.bfloat16
I32 = jnp.int32
VMEM = pltpu.VMEM

NT = (((1,), (1,)), ((), ()))
NN = (((1,), (0,)), ((), ()))

N_BY = 8
Y1 = 144
K_TAPS = 9 * 384


def dot(a, b, dims=NN):
    return lax.dot_general(a, b, dims, preferred_element_type=F32)


def leaky(u):
    return jnp.where(u > 0, u, 0.1 * u)


def split2(v):
    high = v.astype(BF16)
    return high, (v - high.astype(F32)).astype(BF16)


def pack_kernel(dest_ref, cell_ref, value_ref, out_ref):
    rows = dest_ref.shape[1]
    step = 256
    brick = lax.broadcasted_iota(I32, (128, step), 0)
    before = (
        lax.broadcasted_iota(I32, (step, step), 0) < lax.broadcasted_iota(I32, (step, step), 1)
    ).astype(F32).astype(BF16)
    slot_ids = lax.broadcasted_iota(I32, (32, step), 0)
    seen = jnp.zeros((128, 1), F32)
    total = jnp.zeros((128, 256), F32)
    for start in range(0, rows, step):
        here = slice(start, start + step)
        hot = (brick == dest_ref[:, here]).astype(F32)
        hot_b = hot.astype(BF16)
        prefix = dot(hot_b, before) + seen
        slot = jnp.sum(hot * prefix, axis=0, keepdims=True).astype(I32)
        seen = prefix[:, step - 1 :] + hot[:, step - 1 :]
        mine = slot_ids == slot
        pieces = [cell_ref[:, here].astype(F32)] + [value_ref[f : f + 1, here] for f in range(3)]
        highs, lows = [], []
        for piece in pieces:
            high = piece.astype(BF16).astype(F32)
            highs.append(jnp.where(mine, high, 0.0))
            lows.append(jnp.where(mine, piece - high, 0.0))
        spread = jnp.concatenate(highs + lows, axis=0).astype(BF16)
        total = total + dot(hot_b, spread, NT)
    table = total[:, :128] + total[:, 128:]
    for k, shifted in enumerate(
        (
            table,
            jnp.concatenate([table[128 - N_BY :], table[: 128 - N_BY]], axis=0),
            jnp.concatenate([table[N_BY:], table[:N_BY]], axis=0),
        )
    ):
        out_ref[:, k, :] = shifted


def pack(dest, cell, values):
    return pl.pallas_call(
        pack_kernel,
        out_shape=jax.ShapeDtypeStruct((128, 3, 128), F32),
        name="pack",
    )(dest, cell, values)


def paint_kernel(in_ref, after_any, out_ref, first_ref, last_ref, acc_ref):
    z_ids = lax.broadcasted_iota(I32, (16, 128), 0)
    blank = jnp.zeros((16, 128), F32)
    group = 8
    for table, base, shift, rows in ((1, 0, 256, 256), (0, 256, 0, 512), (2, 768, 0, 256)):
        turned = jnp.transpose(in_ref[:, table, :], (1, 0))
        cells = turned[0:32].astype(I32)
        place = ((cells >> 8) & 3) * 128 + (cells & 127) - shift
        code = ((cells >> 7) & 1) * 16 + (cells >> 10)
        parts = []
        for f in range(3):
            value = turned[32 + 32 * f : 64 + 32 * f]
            high = value.astype(BF16).astype(F32)
            parts.append((high, value - high))
        place_ids = lax.broadcasted_iota(I32, (rows, 128), 0)
        for start in range(0, 32, group):
            hots, sides = [], []
            for s in range(start, start + group):
                hots.append((place_ids == place[s : s + 1]).astype(F32).astype(BF16))
                column = []
                for part in range(2):
                    for par in range(2):
                        here = z_ids + par * 16 == code[s : s + 1]
                        for f in range(3):
                            column.append(jnp.where(here, parts[f][part][s : s + 1], 0.0))
                        column.append(blank)
                sides.append(jnp.concatenate(column, axis=0).astype(BF16))
            added = dot(jnp.concatenate(hots, axis=1), jnp.concatenate(sides, axis=1), NT)
            if start == 0:
                acc_ref[base : base + rows] = added
            else:
                acc_ref[base : base + rows] += added
    painted = (acc_ref[:, :128] + acc_ref[:, 128:]).reshape(8, 128, 128)
    out_ref[...] = painted.astype(BF16)
    first_ref[...] = painted[:, 0:8].astype(BF16)
    last_ref[...] = painted[:, 120:128].astype(BF16)


def paint(incoming, after):
    edge = jax.ShapeDtypeStruct((8, 8, 128), BF16)
    return pl.pallas_call(
        paint_kernel,
        in_specs=[pl.BlockSpec(memory_space=pltpu.VMEM), pl.BlockSpec(memory_space=pl.ANY)],
        out_shape=(jax.ShapeDtypeStruct((8, 128, 128), BF16), edge, edge),
        scratch_shapes=[VMEM((1024, 256), F32)],
        name="paint",
    )(incoming, after)


def weights_kernel(win_ref, r1_ref):
    lane = lax.broadcasted_iota(I32, (16, 128), 1)
    depth = lax.broadcasted_iota(I32, (16, 128), 0)
    blank = jnp.zeros((16, 128), F32)
    hits = []
    for tile in range(8):
        first_z = 14 + 4 * tile if tile < 4 else 13 + 4 * (tile - 4)
        tap_z = (depth - first_z - 2 * (lane // 64) + 49) % 16
        hits.append([tap_z == tz for tz in range(3)])
    for tx in range(3):
        for ty in range(3):
            rows = [
                [
                    jnp.broadcast_to(
                        jnp.concatenate([win_ref[tx, tz * 3 + f, ty : ty + 1, :].astype(F32)] * 2, axis=1),
                        (16, 128),
                    )
                    for tz in range(3)
                ]
                for f in range(3)
            ]
            for tile in range(8):
                column = []
                for f in range(3):
                    block = blank
                    for tz in range(3):
                        block = jnp.where(hits[tile][tz], rows[f][tz], block)
                    column.append(block)
                block = jnp.concatenate(column + [blank], axis=0).astype(BF16)
                for out in range(2):
                    at = ty * 256 + (tx + out) * 64
                    r1_ref[out * 8 + tile, at : at + 64] = block
    none = jnp.zeros((64, 128), BF16)
    for ty in range(3):
        for tile in range(8):
            r1_ref[tile, ty * 256 + 192 : ty * 256 + 256] = none
            r1_ref[8 + tile, ty * 256 : ty * 256 + 64] = none


def late_weights_kernel(wmid_ref, wout_ref, w2_ref, w3_ref):
    low = lax.broadcasted_iota(I32, (64, 128), 1) < 64
    zero = jnp.zeros((64, 128), F32)
    for source, target, window in ((wmid_ref, w2_ref, (0, 1, 2, 3, 4, 5)), (wout_ref, w3_ref, (0, 1, 3, 2, 4, 5))):
        for tap in range(9):
            front = source[tap // 3, tap % 3, :, 0:128].astype(F32)
            back = jnp.concatenate(
                [source[tap // 3, tap % 3, :, 128:192].astype(F32), jnp.zeros((64, 64), F32)], axis=1
            )
            front = jnp.transpose(jnp.concatenate([front, front], axis=0), (1, 0))
            back = jnp.transpose(jnp.concatenate([back, back], axis=0), (1, 0))
            taps = (front[0:64], front[64:128], back[0:64])
            for at, w in enumerate(window):
                rows = slice(tap * 384 + at * 64, tap * 384 + at * 64 + 64)
                for h in range(2):
                    a = taps[w - 2 * h] if 0 <= w - 2 * h < 3 else zero
                    b = taps[w - 2 * h - 1] if 0 <= w - 2 * h - 1 < 3 else zero
                    natural = jnp.where(low, a, b).astype(BF16)
                    if target is w2_ref:
                        target[h, rows] = jnp.where(low, b, a).astype(BF16)
                        target[2 + h, rows] = natural
                    else:
                        target[h, rows] = natural


def weights(win):
    return pl.pallas_call(
        weights_kernel,
        out_shape=jax.ShapeDtypeStruct((16, 768, 128), BF16),
        name="weights",
    )(win)


def late_weights(wmid, wout):
    return pl.pallas_call(
        late_weights_kernel,
        out_shape=(
            jax.ShapeDtypeStruct((4, K_TAPS, 128), BF16),
            jax.ShapeDtypeStruct((2, K_TAPS, 128), BF16),
        ),
        name="late_weights",
    )(wmid, wout)


def layers_kernel(
    painted_ref, top_ref, bottom_ref, r1_any, w2_any, w3_any, out_any,
    r1_ref, w2_ref, w3_ref, ext_ref, v1_ref, tmp_ref, first_ref, second_ref, rows_ref, third_ref, out_ref,
    in_sem, out_sem,
):
    copies = [
        pltpu.make_async_copy(a, b, in_sem.at[i])
        for i, (a, b) in enumerate(((r1_any, r1_ref), (w2_any, w2_ref), (w3_any, w3_ref)))
    ]
    copies[0].start()
    ext_ref[:, 144:160] = jnp.zeros((8, 16, 128), F32)
    tmp_ref[:, :, Y1:152] = jnp.zeros((2, 7, 8, 128), F32)
    ext_ref[:, 0:8] = top_ref[...].astype(F32)
    ext_ref[:, 136:144] = bottom_ref[...].astype(F32)
    ext_ref[:, 8:136] = painted_ref[...].astype(F32)
    for ty in range(3):
        for pair in range(8):
            v1_ref[ty, pair * Y1 : pair * Y1 + Y1] = ext_ref[pair, 4 + ty : 4 + ty + Y1].astype(BF16)
    copies[0].wait()
    copies[1].start()
    copies[2].start()

    def first_columns(column, carry):
        lhs = jnp.concatenate(
            [v1_ref[ty, p * Y1 : p * Y1 + 7 * Y1] for ty in range(3) for p in range(2)], axis=1
        )
        rhs = jnp.concatenate([r1_ref[2 * column], r1_ref[2 * column + 1]], axis=1)
        u = leaky(dot(lhs, rhs))
        for h in range(2):
            tmp_ref[h, :, 0:Y1] = u[:, h * 128 : h * 128 + 128].reshape(7, Y1, 128)
        out = column // 4
        for h in range(2):
            tile = (column % 4) * 2 + h
            for m in range(7):
                row = pl.multiple_of((2 * m + out) * Y1, Y1)
                for s in range(3):
                    first_ref[s, tile, pl.ds(row, Y1)] = tmp_ref[h, m, 2 * s : 2 * s + Y1].astype(BF16)
        return carry

    lax.fori_loop(0, 8, first_columns, 0)
    copies[1].wait()

    low = lax.broadcasted_iota(I32, (5 * Y1, 128), 1) < 64

    def second_rows(step, carry):
        group = step // 2
        b = step % 2
        outs = []
        for parity in range(2):
            pieces = []
            for tx in range(3):
                row = pl.multiple_of((group * 5 + 2 * tx) * Y1, Y1)
                for ty in range(3):
                    for w in range(3):
                        tile = parity * 4 + (2 * b + w) % 4
                        pieces.append(first_ref[ty, tile, pl.ds(row, 5 * Y1)])
            rhs = jnp.concatenate([w2_ref[2 * parity], w2_ref[2 * parity + 1]], axis=1)
            outs.append(leaky(dot(jnp.concatenate(pieces, axis=1), rhs)))
        even, odd = outs
        for h in range(2):
            e = even[:, h * 128 : h * 128 + 128]
            o = odd[:, h * 128 : h * 128 + 128]
            for k, merged in enumerate((jnp.where(low, o, e), jnp.where(low, e, o))):
                tmp_ref[k, 0:5, 0:Y1] = merged.reshape(5, Y1, 128)
            for k in range(2):
                tile = 4 * b + 2 * h + k
                for q in range(5):
                    row = pl.multiple_of((group * 5 + q) * 128, 128)
                    for s in range(3):
                        second_ref[s, tile, pl.ds(row, 128)] = tmp_ref[k, q, s : s + 128].astype(BF16)
        return carry

    lax.fori_loop(0, 4, second_rows, 0)
    copies[2].wait()

    def third_rows(b):
        pieces = []
        for tx in range(3):
            for ty in range(3):
                for w in range(3):
                    pieces.append(second_ref[ty, (2 * b + w) % 8, tx * 128 : tx * 128 + 1024])
        rhs = jnp.concatenate([w3_ref[0], w3_ref[1]], axis=1)
        u = leaky(dot(jnp.concatenate(pieces, axis=1), rhs))
        for h in range(2):
            rows_ref[b % 2, h] = u[:, h * 128 : h * 128 + 128]

    def third_planes(b):
        for x in range(8):
            for h in range(2):
                turned = jnp.transpose(rows_ref[b % 2, h, x * 128 : x * 128 + 128], (1, 0))
                for k in range(2):
                    third_ref[2 * h + k, pl.ds(x, 64, stride=8), :] = turned[64 * k : 64 * k + 64]
        for j in range(4):
            out_ref[4 * b + j] = third_ref[j].astype(BF16)
        copy = pltpu.make_async_copy(
            out_ref.at[4 * b : 4 * b + 4], out_any.at[4 * b : 4 * b + 4], out_sem.at[b]
        )
        copy.start()
        return copy

    sent = []
    for b in range(4):
        third_rows(b)
        if b:
            sent.append(third_planes(b - 1))
    sent.append(third_planes(3))
    for copy in sent:
        copy.wait()


def layers(painted, top, bottom, r1, w2, w3):
    whole = pl.BlockSpec(memory_space=pltpu.VMEM)
    anywhere = pl.BlockSpec(memory_space=pl.ANY)
    return pl.pallas_call(
        layers_kernel,
        in_specs=[whole] * 3 + [anywhere] * 3,
        out_specs=anywhere,
        out_shape=jax.ShapeDtypeStruct((16, 512, 128), BF16),
        scratch_shapes=[
            VMEM((16, 768, 128), BF16),
            VMEM((4, K_TAPS, 128), BF16),
            VMEM((2, K_TAPS, 128), BF16),
            VMEM((8, 160, 128), F32),
            VMEM((3, 8 * Y1, 128), BF16),
            VMEM((2, 7, 152, 128), F32),
            VMEM((3, 8, 14 * Y1, 128), BF16),
            VMEM((3, 8, 10 * 128, 128), BF16),
            VMEM((2, 2, 1024, 128), F32),
            VMEM((4, 512, 128), F32),
            VMEM((16, 512, 128), BF16),
            pltpu.SemaphoreType.DMA((3,)),
            pltpu.SemaphoreType.DMA((4,)),
        ],
        compiler_params=pltpu.CompilerParams(vmem_limit_bytes=60 << 20),
        name="layers",
    )(painted, top, bottom, r1, w2, w3)


def twiddle_rows(count):
    position = np.arange(count, dtype=np.int64)
    phase = position[:, None] * position[None, :] % count
    angle = phase.astype(np.float32) * np.float32(2.0 * math.pi / count)
    factor = np.float32(1.0 / math.sqrt(count))
    parts = np.stack([np.cos(angle) * factor, -np.sin(angle) * factor])
    parts = parts.reshape(2 * count, count // 8, 8)
    table = np.zeros((2, 2 * count, count // 8, 2, 8), np.float32)
    for parity in range(2):
        table[parity, :, :, parity, :] = parts
    return table.reshape(4 * count, 2, count).transpose(1, 0, 2)


def transform_kernel(twiddle_ref, in_any, out_any, in_ref, out_ref, in_sem, out_sem):
    chunks = 8
    rows = 512 // chunks
    channels = 64 // chunks
    arrivals = []
    for i in range(chunks):
        here = slice(i * rows, i * rows + rows)
        copy = pltpu.make_async_copy(in_any.at[:, here], in_ref.at[:, here], in_sem.at[i])
        copy.start()
        arrivals.append(copy)
    lhs = jnp.concatenate([twiddle_ref[0], twiddle_ref[1]], axis=1)
    sent = []
    for i in range(chunks):
        arrivals[i].wait()
        for pair in range(channels // 4):
            at = i * rows + pair * 32
            rhs = jnp.concatenate(
                [in_ref[:, at + k * 16 : at + k * 16 + 16].reshape(256, 128) for k in range(2)], axis=1
            )
            u = dot(lhs, rhs).astype(BF16)
            for k in range(2):
                for parity in range(2):
                    for t in range(2):
                        row = (parity * 2 + t) * 128
                        out_ref[t, i * channels + 4 * pair + 2 * k + parity, 0] = (
                            u[row : row + 128, k * 128 : k * 128 + 128]
                        )
        here = slice(i * channels, i * channels + channels)
        copy = pltpu.make_async_copy(out_ref.at[:, here], out_any.at[:, here], out_sem.at[i])
        copy.start()
        sent.append(copy)
    for copy in sent:
        copy.wait()


def transform(twiddle, moved):
    anywhere = pl.BlockSpec(memory_space=pl.ANY)
    return pl.pallas_call(
        transform_kernel,
        in_specs=[pl.BlockSpec(memory_space=pltpu.VMEM), anywhere],
        out_specs=anywhere,
        out_shape=jax.ShapeDtypeStruct((2, 64, 1, 128, 128), BF16),
        scratch_shapes=[
            VMEM((16, 512, 128), BF16),
            VMEM((2, 64, 1, 128, 128), BF16),
            pltpu.SemaphoreType.DMA((8,)),
            pltpu.SemaphoreType.DMA((8,)),
        ],
        name="transform",
    )(twiddle, moved)


def on_device(particle_values, destination, cell_index, weight_in, weight_mid, weight_out):
    count_x = lax.axis_size("bx")
    count_y = lax.axis_size("by")
    up_y = [(i, (i + 1) % count_y) for i in range(count_y)]
    down_y = [((i + 1) % count_y, i) for i in range(count_y)]

    outgoing = pack(destination.reshape(1, -1), cell_index.reshape(1, -1), particle_values)
    incoming = lax.all_to_all(outgoing, ("bx", "by"), split_axis=0, concat_axis=0, tiled=True)

    r1 = weights(jnp.transpose(weight_in, (0, 3, 1, 2)))
    painted, first_y, last_y = paint(incoming, r1)
    top = lax.ppermute(last_y, "by", up_y)
    bottom = lax.ppermute(first_y, "by", down_y)
    w2, w3 = late_weights(weight_mid, weight_out)
    third = layers(painted, top, bottom, r1, w2, w3)
    moved = lax.all_to_all(third, "bx", split_axis=0, concat_axis=0, tiled=True)
    twiddle = jnp.asarray(twiddle_rows(count_x * 8), BF16)
    return transform(twiddle, moved)


def solution(mesh):
    placed = (P(None, ("bx", "by")), P(("bx", "by"), None), P(("bx", "by")), P(), P(), P())
    return jax.shard_map(
        on_device,
        mesh=mesh,
        in_specs=placed,
        out_specs=P(None, None, "bx", None, "by"),
        check_vma=False,
    )
```

```python
import math

import jax
import jax.numpy as jnp
import numpy as np
from jax import lax
from jax.experimental import pallas as pl
from jax.experimental.pallas import tpu as pltpu
from jax.sharding import PartitionSpec as P

F32 = jnp.float32
BF16 = jnp.bfloat16
I32 = jnp.int32
VMEM = pltpu.VMEM

NT = (((1,), (1,)), ((), ()))
NN = (((1,), (0,)), ((), ()))

N_BY = 8
Y1 = 144
K_TAPS = 9 * 384


def dot(a, b, dims=NN):
    return lax.dot_general(a, b, dims, preferred_element_type=F32)


def leaky(u):
    return jnp.where(u > 0, u, 0.1 * u)


def split2(v):
    high = v.astype(BF16)
    return high, (v - high.astype(F32)).astype(BF16)


def pack_kernel(dest_ref, cell_ref, value_ref, out_ref):
    rows = dest_ref.shape[1]
    step = 256
    brick = lax.broadcasted_iota(I32, (128, step), 0)
    before = (
        lax.broadcasted_iota(I32, (step, step), 0) < lax.broadcasted_iota(I32, (step, step), 1)
    ).astype(F32).astype(BF16)
    slot_ids = lax.broadcasted_iota(I32, (32, step), 0)
    seen = jnp.zeros((128, 1), F32)
    total = jnp.zeros((128, 256), F32)
    for start in range(0, rows, step):
        here = slice(start, start + step)
        hot = (brick == dest_ref[:, here]).astype(F32)
        hot_b = hot.astype(BF16)
        prefix = dot(hot_b, before) + seen
        slot = jnp.sum(hot * prefix, axis=0, keepdims=True).astype(I32)
        seen = prefix[:, step - 1 :] + hot[:, step - 1 :]
        mine = slot_ids == slot
        pieces = [cell_ref[:, here].astype(F32)] + [value_ref[f : f + 1, here] for f in range(3)]
        highs, lows = [], []
        for piece in pieces:
            high = piece.astype(BF16).astype(F32)
            highs.append(jnp.where(mine, high, 0.0))
            lows.append(jnp.where(mine, piece - high, 0.0))
        spread = jnp.concatenate(highs + lows, axis=0).astype(BF16)
        total = total + dot(hot_b, spread, NT)
    table = total[:, :128] + total[:, 128:]
    for k, shifted in enumerate(
        (
            table,
            jnp.concatenate([table[128 - N_BY :], table[: 128 - N_BY]], axis=0),
            jnp.concatenate([table[N_BY:], table[:N_BY]], axis=0),
        )
    ):
        out_ref[:, k, :] = shifted


def pack(dest, cell, values):
    return pl.pallas_call(
        pack_kernel,
        out_shape=jax.ShapeDtypeStruct((128, 3, 128), F32),
        name="pack",
    )(dest, cell, values)


def paint_kernel(in_ref, after_any, out_ref, first_ref, last_ref, acc_ref):
    z_ids = lax.broadcasted_iota(I32, (16, 128), 0).astype(F32).astype(BF16)
    y_ids = lax.broadcasted_iota(I32, (128, 128), 0).astype(F32).astype(BF16)
    one = jnp.ones((16, 128), BF16)
    blank = jnp.zeros((16, 128), BF16)
    group = 8

    def spread(row):
        return jnp.broadcast_to(row, (16, 128)).astype(BF16)

    for table, base, pairs in ((1, 0, (2, 3)), (0, 256, (0, 1, 2, 3)), (2, 768, (0, 1))):
        turned = jnp.transpose(in_ref[:, table, :], (1, 0))
        cells = turned[0:32].astype(I32)
        pair = ((cells >> 8) & 3).astype(F32)
        y = (cells & 127).astype(F32)
        code = (((cells >> 7) & 1) * 16 + (cells >> 10)).astype(F32)
        parts = []
        for f in range(3):
            value = turned[32 + 32 * f : 64 + 32 * f]
            high = value.astype(BF16).astype(F32)
            parts.append((high, value - high))
        rows = 128 * len(pairs)
        for start in range(0, 32, group):
            hots, sides = [], []
            for s in range(start, start + group):
                along_y = jnp.where(
                    y_ids == jnp.concatenate([spread(y[s : s + 1])] * 8, axis=0),
                    jnp.concatenate([one] * 8, axis=0),
                    jnp.concatenate([blank] * 8, axis=0),
                )
                my_pair = spread(pair[s : s + 1])
                hots.append(
                    jnp.concatenate(
                        [
                            along_y
                            * jnp.concatenate(
                                [jnp.where(my_pair == jnp.full((16, 128), p, BF16), one, blank)] * 8, axis=0
                            )
                            for p in pairs
                        ],
                        axis=0,
                    )
                )
                my_code = spread(code[s : s + 1])
                column = []
                for part in range(2):
                    values = [spread(parts[f][part][s : s + 1]) for f in range(3)]
                    for par in range(2):
                        here = z_ids + jnp.full((16, 128), par * 16, BF16) == my_code
                        for f in range(3):
                            column.append(jnp.where(here, values[f], blank))
                        column.append(blank)
                sides.append(jnp.concatenate(column, axis=0))
            added = dot(jnp.concatenate(hots, axis=1), jnp.concatenate(sides, axis=1), NT)
            if start == 0:
                acc_ref[base : base + rows] = added
            else:
                acc_ref[base : base + rows] += added
    painted = (acc_ref[:, :128] + acc_ref[:, 128:]).reshape(8, 128, 128)
    out_ref[...] = painted.astype(BF16)
    first_ref[...] = painted[:, 0:8].astype(BF16)
    last_ref[...] = painted[:, 120:128].astype(BF16)


def paint(incoming, after):
    edge = jax.ShapeDtypeStruct((8, 8, 128), BF16)
    return pl.pallas_call(
        paint_kernel,
        in_specs=[pl.BlockSpec(memory_space=pltpu.VMEM), pl.BlockSpec(memory_space=pl.ANY)],
        out_shape=(jax.ShapeDtypeStruct((8, 128, 128), BF16), edge, edge),
        scratch_shapes=[VMEM((1024, 256), F32)],
        name="paint",
    )(incoming, after)


def weights_kernel(win_ref, wmid_ref, r1_ref, w2_ref):
    lane = lax.broadcasted_iota(I32, (16, 128), 1)
    depth = lax.broadcasted_iota(I32, (16, 128), 0)
    blank = jnp.zeros((16, 128), F32)
    hits = []
    for tile in range(8):
        first_z = 14 + 4 * tile if tile < 4 else 13 + 4 * (tile - 4)
        tap_z = (depth - first_z - 2 * (lane // 64) + 49) % 16
        hits.append([tap_z == tz for tz in range(3)])
    for tx in range(3):
        for ty in range(3):
            rows = [
                [
                    jnp.broadcast_to(
                        jnp.concatenate([win_ref[tx, tz * 3 + f, ty : ty + 1, :].astype(F32)] * 2, axis=1),
                        (16, 128),
                    )
                    for tz in range(3)
                ]
                for f in range(3)
            ]
            for tile in range(8):
                column = []
                for f in range(3):
                    block = blank
                    for tz in range(3):
                        block = jnp.where(hits[tile][tz], rows[f][tz], block)
                    column.append(block)
                block = jnp.concatenate(column + [blank], axis=0).astype(BF16)
                for out in range(2):
                    at = ty * 256 + (tx + out) * 64
                    r1_ref[out * 8 + tile, at : at + 64] = block
    none = jnp.zeros((64, 128), BF16)
    for ty in range(3):
        for tile in range(8):
            r1_ref[tile, ty * 256 + 192 : ty * 256 + 256] = none
            r1_ref[8 + tile, ty * 256 : ty * 256 + 64] = none
    tap_rows(wmid_ref, w2_ref, (0, 1, 2, 3, 4, 5), True)


def tap_rows(source, target, window, swapped):
    low = lax.broadcasted_iota(I32, (64, 128), 1) < 64
    zero = jnp.zeros((64, 128), F32)
    for tap in range(9):
        front = source[tap // 3, tap % 3, :, 0:128].astype(F32)
        back = jnp.concatenate(
            [source[tap // 3, tap % 3, :, 128:192].astype(F32), jnp.zeros((64, 64), F32)], axis=1
        )
        front = jnp.transpose(jnp.concatenate([front, front], axis=0), (1, 0))
        back = jnp.transpose(jnp.concatenate([back, back], axis=0), (1, 0))
        taps = (front[0:64], front[64:128], back[0:64])
        for at, w in enumerate(window):
            rows = slice(tap * 384 + at * 64, tap * 384 + at * 64 + 64)
            for h in range(2):
                a = taps[w - 2 * h] if 0 <= w - 2 * h < 3 else zero
                b = taps[w - 2 * h - 1] if 0 <= w - 2 * h - 1 < 3 else zero
                if swapped:
                    target[2 + h, rows] = jnp.where(low, b, a).astype(BF16)
                target[h, rows] = jnp.where(low, a, b).astype(BF16)


def late_weights_kernel(wout_ref, w3_ref):
    tap_rows(wout_ref, w3_ref, (0, 1, 3, 2, 4, 5), False)


def weights(win, wmid):
    return pl.pallas_call(
        weights_kernel,
        out_shape=(
            jax.ShapeDtypeStruct((16, 768, 128), BF16),
            jax.ShapeDtypeStruct((4, K_TAPS, 128), BF16),
        ),
        name="weights",
    )(win, wmid)


def late_weights(wout):
    return pl.pallas_call(
        late_weights_kernel,
        out_shape=jax.ShapeDtypeStruct((2, K_TAPS, 128), BF16),
        name="late_weights",
    )(wout)


def layers_kernel(
    painted_ref, top_ref, bottom_ref, r1_ref, w2_ref, w3_ref, out_any,
    ext_ref, v1_ref, tmp_ref, first_ref, second_ref, rows_ref, third_ref, out_ref, out_sem,
):
    ext_ref[:, 144:160] = jnp.zeros((8, 16, 128), F32)
    tmp_ref[:, :, Y1:152] = jnp.zeros((2, 7, 8, 128), F32)
    ext_ref[:, 0:8] = top_ref[...].astype(F32)
    ext_ref[:, 136:144] = bottom_ref[...].astype(F32)
    ext_ref[:, 8:136] = painted_ref[...].astype(F32)
    for ty in range(3):
        for pair in range(8):
            v1_ref[ty, pair * Y1 : pair * Y1 + Y1] = ext_ref[pair, 4 + ty : 4 + ty + Y1].astype(BF16)

    def first_columns(column, carry):
        lhs = jnp.concatenate(
            [v1_ref[ty, p * Y1 : p * Y1 + 7 * Y1] for ty in range(3) for p in range(2)], axis=1
        )
        rhs = jnp.concatenate([r1_ref[2 * column], r1_ref[2 * column + 1]], axis=1)
        u = leaky(dot(lhs, rhs))
        for h in range(2):
            tmp_ref[h, :, 0:Y1] = u[:, h * 128 : h * 128 + 128].reshape(7, Y1, 128)
        out = column // 4
        for h in range(2):
            tile = (column % 4) * 2 + h
            for m in range(7):
                row = pl.multiple_of((2 * m + out) * Y1, Y1)
                for s in range(3):
                    first_ref[s, tile, pl.ds(row, Y1)] = tmp_ref[h, m, 2 * s : 2 * s + Y1].astype(BF16)
        return carry

    lax.fori_loop(0, 8, first_columns, 0)

    low = lax.broadcasted_iota(I32, (5 * Y1, 128), 1) < 64

    def second_rows(step, carry):
        group = step // 2
        b = step % 2
        outs = []
        for parity in range(2):
            pieces = []
            for tx in range(3):
                row = pl.multiple_of((group * 5 + 2 * tx) * Y1, Y1)
                for ty in range(3):
                    for w in range(3):
                        tile = parity * 4 + (2 * b + w) % 4
                        pieces.append(first_ref[ty, tile, pl.ds(row, 5 * Y1)])
            rhs = jnp.concatenate([w2_ref[2 - 2 * parity], w2_ref[3 - 2 * parity]], axis=1)
            outs.append(leaky(dot(jnp.concatenate(pieces, axis=1), rhs)))
        even, odd = outs
        for h in range(2):
            e = even[:, h * 128 : h * 128 + 128]
            o = odd[:, h * 128 : h * 128 + 128]
            for k, merged in enumerate((jnp.where(low, o, e), jnp.where(low, e, o))):
                tmp_ref[k, 0:5, 0:Y1] = merged.reshape(5, Y1, 128)
            for k in range(2):
                tile = 4 * b + 2 * h + k
                for q in range(5):
                    row = pl.multiple_of((group * 5 + q) * 128, 128)
                    for s in range(3):
                        second_ref[s, tile, pl.ds(row, 128)] = tmp_ref[k, q, s : s + 128].astype(BF16)
        return carry

    lax.fori_loop(0, 4, second_rows, 0)

    def third_rows(b):
        pieces = []
        for tx in range(3):
            for ty in range(3):
                for w in range(3):
                    pieces.append(second_ref[ty, (2 * b + w) % 8, tx * 128 : tx * 128 + 1024])
        rhs = jnp.concatenate([w3_ref[0], w3_ref[1]], axis=1)
        u = leaky(dot(jnp.concatenate(pieces, axis=1), rhs))
        for h in range(2):
            rows_ref[b % 2, h] = u[:, h * 128 : h * 128 + 128]

    def third_planes(b):
        for x in range(8):
            for h in range(2):
                turned = jnp.transpose(rows_ref[b % 2, h, x * 128 : x * 128 + 128], (1, 0))
                for k in range(2):
                    third_ref[2 * h + k, pl.ds(x, 64, stride=8), :] = turned[64 * k : 64 * k + 64]
        for j in range(4):
            out_ref[4 * b + j] = third_ref[j].astype(BF16)
        copy = pltpu.make_async_copy(
            out_ref.at[4 * b : 4 * b + 4], out_any.at[4 * b : 4 * b + 4], out_sem.at[b]
        )
        copy.start()
        return copy

    sent = []
    for b in range(4):
        third_rows(b)
        if b:
            sent.append(third_planes(b - 1))
    sent.append(third_planes(3))
    for copy in sent:
        copy.wait()


def layers(painted, top, bottom, r1, w2, w3):
    whole = pl.BlockSpec(memory_space=pltpu.VMEM)
    anywhere = pl.BlockSpec(memory_space=pl.ANY)
    return pl.pallas_call(
        layers_kernel,
        in_specs=[whole] * 6,
        out_specs=anywhere,
        out_shape=jax.ShapeDtypeStruct((16, 512, 128), BF16),
        scratch_shapes=[
            VMEM((8, 160, 128), F32),
            VMEM((3, 8 * Y1, 128), BF16),
            VMEM((2, 7, 152, 128), F32),
            VMEM((3, 8, 14 * Y1, 128), BF16),
            VMEM((3, 8, 10 * 128, 128), BF16),
            VMEM((2, 2, 1024, 128), F32),
            VMEM((4, 512, 128), F32),
            VMEM((16, 512, 128), BF16),
            pltpu.SemaphoreType.DMA((4,)),
        ],
        compiler_params=pltpu.CompilerParams(vmem_limit_bytes=44 << 20),
        name="layers",
    )(painted, top, bottom, r1, w2, w3)


def twiddle_rows(count):
    position = np.arange(count, dtype=np.int64)
    phase = position[:, None] * position[None, :] % count
    angle = phase.astype(np.float32) * np.float32(2.0 * math.pi / count)
    factor = np.float32(1.0 / math.sqrt(count))
    parts = np.stack([np.cos(angle) * factor, -np.sin(angle) * factor])
    parts = parts.reshape(2 * count, count // 8, 8)
    table = np.zeros((2, 2 * count, count // 8, 2, 8), np.float32)
    for parity in range(2):
        table[parity, :, :, parity, :] = parts
    return table.reshape(4 * count, 2, count).transpose(1, 0, 2)


def transform_kernel(twiddle_ref, in_ref, out_ref):
    lhs = jnp.concatenate([twiddle_ref[0], twiddle_ref[1]], axis=1)
    base = pl.multiple_of(pl.program_id(0) * 256, 256)
    for pair in range(8):
        rhs = jnp.concatenate(
            [
                in_ref[:, pl.ds(base + (2 * pair + k) * 16, 16)].reshape(256, 128)
                for k in range(2)
            ],
            axis=1,
        )
        u = dot(lhs, rhs).astype(BF16)
        for k in range(2):
            for parity in range(2):
                for t in range(2):
                    at = (parity * 2 + t) * 128
                    out_ref[t, 4 * pair + 2 * k + parity, 0] = u[at : at + 128, k * 128 : k * 128 + 128]


def transform(twiddle, moved):
    return pl.pallas_call(
        transform_kernel,
        grid=(2,),
        in_specs=[
            pl.BlockSpec((2, 512, 128), lambda i: (0, 0, 0)),
            pl.BlockSpec(memory_space=pltpu.VMEM),
        ],
        out_specs=pl.BlockSpec((2, 32, 1, 128, 128), lambda i: (0, i, 0, 0, 0)),
        out_shape=jax.ShapeDtypeStruct((2, 64, 1, 128, 128), BF16),
        name="transform",
    )(twiddle, moved)


def in_vmem(value):
    return pltpu.with_memory_space_constraint(value, pltpu.VMEM)


def on_device(particle_values, destination, cell_index, weight_in, weight_mid, weight_out):
    count_x = lax.axis_size("bx")
    count_y = lax.axis_size("by")
    up_y = [(i, (i + 1) % count_y) for i in range(count_y)]
    down_y = [((i + 1) % count_y, i) for i in range(count_y)]

    outgoing = pack(destination.reshape(1, -1), cell_index.reshape(1, -1), particle_values)
    incoming = lax.all_to_all(outgoing, ("bx", "by"), split_axis=0, concat_axis=0, tiled=True)

    r1, w2 = weights(jnp.transpose(weight_in, (0, 3, 1, 2)), weight_mid)
    incoming = in_vmem(incoming)
    painted, first_y, last_y = paint(incoming, r1)
    top = lax.ppermute(last_y, "by", up_y)
    bottom = lax.ppermute(first_y, "by", down_y)
    w3 = late_weights(weight_out)
    third = layers(*(in_vmem(v) for v in (painted, top, bottom, r1, w2, w3)))
    moved = lax.all_to_all(third, "bx", split_axis=0, concat_axis=0, tiled=True)
    twiddle = jnp.asarray(twiddle_rows(count_x * 8), BF16)
    return transform(twiddle, in_vmem(moved))


def solution(mesh):
    placed = (P(None, ("bx", "by")), P(("bx", "by"), None), P(("bx", "by")), P(), P(), P())
    return jax.shard_map(
        on_device,
        mesh=mesh,
        in_specs=placed,
        out_specs=P(None, None, "bx", None, "by"),
        check_vma=False,
    )
```

```python
import math

import jax
import jax.numpy as jnp
import numpy as np
from jax import lax
from jax.experimental import pallas as pl
from jax.experimental.pallas import tpu as pltpu
from jax.sharding import PartitionSpec as P

F32 = jnp.float32
BF16 = jnp.bfloat16
I32 = jnp.int32
VMEM = pltpu.VMEM

NT = (((1,), (1,)), ((), ()))
NN = (((1,), (0,)), ((), ()))

N_BY = 8
Y1 = 144
K_TAPS = 9 * 384


def dot(a, b, dims=NN):
    return lax.dot_general(a, b, dims, preferred_element_type=F32)


def leaky(u):
    return jnp.where(u > 0, u, 0.1 * u)


def split2(v):
    high = v.astype(BF16)
    return high, (v - high.astype(F32)).astype(BF16)


def pack_kernel(dest_ref, cell_ref, value_ref, out_ref):
    rows = dest_ref.shape[1]
    step = 256
    brick = lax.broadcasted_iota(I32, (128, step), 0)
    before = (
        lax.broadcasted_iota(I32, (step, step), 0) < lax.broadcasted_iota(I32, (step, step), 1)
    ).astype(F32).astype(BF16)
    slot_ids = lax.broadcasted_iota(I32, (32, step), 0)
    seen = jnp.zeros((128, 1), F32)
    total = jnp.zeros((128, 256), F32)
    for start in range(0, rows, step):
        here = slice(start, start + step)
        hot = (brick == dest_ref[:, here]).astype(F32)
        hot_b = hot.astype(BF16)
        prefix = dot(hot_b, before) + seen
        slot = jnp.sum(hot * prefix, axis=0, keepdims=True).astype(I32)
        seen = prefix[:, step - 1 :] + hot[:, step - 1 :]
        mine = slot_ids == slot
        pieces = [cell_ref[:, here].astype(F32)] + [value_ref[f : f + 1, here] for f in range(3)]
        highs, lows = [], []
        for piece in pieces:
            high = piece.astype(BF16).astype(F32)
            highs.append(jnp.where(mine, high, 0.0))
            lows.append(jnp.where(mine, piece - high, 0.0))
        spread = jnp.concatenate(highs + lows, axis=0).astype(BF16)
        total = total + dot(hot_b, spread, NT)
    table = total[:, :128] + total[:, 128:]
    for k, shifted in enumerate(
        (
            table,
            jnp.concatenate([table[128 - N_BY :], table[: 128 - N_BY]], axis=0),
            jnp.concatenate([table[N_BY:], table[:N_BY]], axis=0),
        )
    ):
        out_ref[:, k, :] = shifted


def pack(dest, cell, values):
    return pl.pallas_call(
        pack_kernel,
        out_shape=jax.ShapeDtypeStruct((128, 3, 128), F32),
        name="pack",
    )(dest, cell, values)


def paint_kernel(in_ref, after_any, out_ref, first_ref, last_ref, acc_ref):
    z_ids = lax.broadcasted_iota(I32, (16, 128), 0).astype(F32).astype(BF16)
    y_ids = lax.broadcasted_iota(I32, (128, 128), 0).astype(F32).astype(BF16)
    one = jnp.ones((16, 128), BF16)
    blank = jnp.zeros((16, 128), BF16)
    group = 8

    def spread(row):
        return jnp.broadcast_to(row, (16, 128)).astype(BF16)

    for table, base, pairs in ((1, 0, (2, 3)), (0, 256, (0, 1, 2, 3)), (2, 768, (0, 1))):
        turned = jnp.transpose(in_ref[:, table, :], (1, 0))
        cells = turned[0:32].astype(I32)
        pair = ((cells >> 8) & 3).astype(F32)
        y = (cells & 127).astype(F32)
        code = (((cells >> 7) & 1) * 16 + (cells >> 10)).astype(F32)
        parts = []
        for f in range(3):
            value = turned[32 + 32 * f : 64 + 32 * f]
            high = value.astype(BF16).astype(F32)
            parts.append((high, value - high))
        rows = 128 * len(pairs)
        for start in range(0, 32, group):
            hots, sides = [], []
            for s in range(start, start + group):
                along_y = jnp.where(
                    y_ids == jnp.concatenate([spread(y[s : s + 1])] * 8, axis=0),
                    jnp.concatenate([one] * 8, axis=0),
                    jnp.concatenate([blank] * 8, axis=0),
                )
                my_pair = spread(pair[s : s + 1])
                hots.append(
                    jnp.concatenate(
                        [
                            along_y
                            * jnp.concatenate(
                                [jnp.where(my_pair == jnp.full((16, 128), p, BF16), one, blank)] * 8, axis=0
                            )
                            for p in pairs
                        ],
                        axis=0,
                    )
                )
                my_code = spread(code[s : s + 1])
                column = []
                for part in range(2):
                    values = [spread(parts[f][part][s : s + 1]) for f in range(3)]
                    for par in range(2):
                        here = z_ids + jnp.full((16, 128), par * 16, BF16) == my_code
                        for f in range(3):
                            column.append(jnp.where(here, values[f], blank))
                        column.append(blank)
                sides.append(jnp.concatenate(column, axis=0))
            added = dot(jnp.concatenate(hots, axis=1), jnp.concatenate(sides, axis=1), NT)
            if start == 0:
                acc_ref[base : base + rows] = added
            else:
                acc_ref[base : base + rows] += added
    painted = (acc_ref[:, :128] + acc_ref[:, 128:]).reshape(8, 128, 128)
    out_ref[...] = painted.astype(BF16)
    first_ref[...] = painted[:, 0:8].astype(BF16)
    last_ref[...] = painted[:, 120:128].astype(BF16)


def paint(incoming, after):
    edge = jax.ShapeDtypeStruct((8, 8, 128), BF16)
    return pl.pallas_call(
        paint_kernel,
        in_specs=[pl.BlockSpec(memory_space=pltpu.VMEM), pl.BlockSpec(memory_space=pl.ANY)],
        out_shape=(VMEM((8, 128, 128), BF16), edge, edge),
        scratch_shapes=[VMEM((1024, 256), F32)],
        name="paint",
    )(incoming, after)


def weights_kernel(win_ref, wmid_ref, r1_ref, w2_ref):
    lane = lax.broadcasted_iota(I32, (16, 128), 1)
    depth = lax.broadcasted_iota(I32, (16, 128), 0)
    blank = jnp.zeros((16, 128), F32)
    hits = []
    for tile in range(8):
        first_z = 14 + 4 * tile if tile < 4 else 13 + 4 * (tile - 4)
        tap_z = (depth - first_z - 2 * (lane // 64) + 49) % 16
        hits.append([tap_z == tz for tz in range(3)])
    for tx in range(3):
        for ty in range(3):
            rows = [
                [
                    jnp.broadcast_to(
                        jnp.concatenate([win_ref[tx, tz * 3 + f, ty : ty + 1, :].astype(F32)] * 2, axis=1),
                        (16, 128),
                    )
                    for tz in range(3)
                ]
                for f in range(3)
            ]
            for tile in range(8):
                column = []
                for f in range(3):
                    block = blank
                    for tz in range(3):
                        block = jnp.where(hits[tile][tz], rows[f][tz], block)
                    column.append(block)
                block = jnp.concatenate(column + [blank], axis=0).astype(BF16)
                for out in range(2):
                    at = ty * 256 + (tx + out) * 64
                    r1_ref[out * 8 + tile, at : at + 64] = block
    none = jnp.zeros((64, 128), BF16)
    for ty in range(3):
        for tile in range(8):
            r1_ref[tile, ty * 256 + 192 : ty * 256 + 256] = none
            r1_ref[8 + tile, ty * 256 : ty * 256 + 64] = none
    tap_rows(wmid_ref, w2_ref, (0, 1, 2, 3, 4, 5), True)


def tap_rows(source, target, window, swapped):
    low = lax.broadcasted_iota(I32, (64, 128), 1) < 64
    zero = jnp.zeros((64, 128), F32)
    for tap in range(9):
        front = source[tap // 3, tap % 3, :, 0:128].astype(F32)
        back = jnp.concatenate(
            [source[tap // 3, tap % 3, :, 128:192].astype(F32), jnp.zeros((64, 64), F32)], axis=1
        )
        front = jnp.transpose(jnp.concatenate([front, front], axis=0), (1, 0))
        back = jnp.transpose(jnp.concatenate([back, back], axis=0), (1, 0))
        taps = (front[0:64], front[64:128], back[0:64])
        for at, w in enumerate(window):
            rows = slice(tap * 384 + at * 64, tap * 384 + at * 64 + 64)
            for h in range(2):
                a = taps[w - 2 * h] if 0 <= w - 2 * h < 3 else zero
                b = taps[w - 2 * h - 1] if 0 <= w - 2 * h - 1 < 3 else zero
                if swapped:
                    target[2 + h, rows] = jnp.where(low, b, a).astype(BF16)
                target[h, rows] = jnp.where(low, a, b).astype(BF16)


def late_weights_kernel(wout_ref, w3_ref):
    tap_rows(wout_ref, w3_ref, (0, 1, 3, 2, 4, 5), False)


def weights(win, wmid):
    return pl.pallas_call(
        weights_kernel,
        out_shape=(
            jax.ShapeDtypeStruct((16, 768, 128), BF16),
            jax.ShapeDtypeStruct((4, K_TAPS, 128), BF16),
        ),
        name="weights",
    )(win, wmid)


def late_weights(wout):
    return pl.pallas_call(
        late_weights_kernel,
        out_shape=VMEM((2, K_TAPS, 128), BF16),
        name="late_weights",
    )(wout)


def layers_kernel(
    painted_ref, top_ref, bottom_ref, r1_ref, w3_ref, w2_any, out_any,
    w2_ref, ext_ref, v1_ref, tmp_ref, first_ref, second_ref, rows_ref, third_ref, out_ref,
    in_sem, out_sem,
):
    arrival = pltpu.make_async_copy(w2_any, w2_ref, in_sem)
    arrival.start()
    ext_ref[:, 144:160] = jnp.zeros((8, 16, 128), F32)
    tmp_ref[:, :, Y1:152] = jnp.zeros((2, 7, 8, 128), F32)
    ext_ref[:, 0:8] = top_ref[...].astype(F32)
    ext_ref[:, 136:144] = bottom_ref[...].astype(F32)
    ext_ref[:, 8:136] = painted_ref[...].astype(F32)
    for ty in range(3):
        for pair in range(8):
            v1_ref[ty, pair * Y1 : pair * Y1 + Y1] = ext_ref[pair, 4 + ty : 4 + ty + Y1].astype(BF16)

    def first_columns(column, carry):
        lhs = jnp.concatenate(
            [v1_ref[ty, p * Y1 : p * Y1 + 7 * Y1] for ty in range(3) for p in range(2)], axis=1
        )
        rhs = jnp.concatenate([r1_ref[2 * column], r1_ref[2 * column + 1]], axis=1)
        u = leaky(dot(lhs, rhs))
        for h in range(2):
            tmp_ref[h, :, 0:Y1] = u[:, h * 128 : h * 128 + 128].reshape(7, Y1, 128)
        out = column // 4
        for h in range(2):
            tile = (column % 4) * 2 + h
            for m in range(7):
                row = pl.multiple_of((2 * m + out) * Y1, Y1)
                for s in range(3):
                    first_ref[s, tile, pl.ds(row, Y1)] = tmp_ref[h, m, 2 * s : 2 * s + Y1].astype(BF16)
        return carry

    lax.fori_loop(0, 8, first_columns, 0)
    arrival.wait()

    low = lax.broadcasted_iota(I32, (5 * Y1, 128), 1) < 64

    def second_rows(step, carry):
        group = step // 2
        b = step % 2
        outs = []
        for parity in range(2):
            pieces = []
            for tx in range(3):
                row = pl.multiple_of((group * 5 + 2 * tx) * Y1, Y1)
                for ty in range(3):
                    for w in range(3):
                        tile = parity * 4 + (2 * b + w) % 4
                        pieces.append(first_ref[ty, tile, pl.ds(row, 5 * Y1)])
            rhs = jnp.concatenate([w2_ref[2 - 2 * parity], w2_ref[3 - 2 * parity]], axis=1)
            outs.append(leaky(dot(jnp.concatenate(pieces, axis=1), rhs)))
        even, odd = outs
        for h in range(2):
            e = even[:, h * 128 : h * 128 + 128]
            o = odd[:, h * 128 : h * 128 + 128]
            for k, merged in enumerate((jnp.where(low, o, e), jnp.where(low, e, o))):
                tmp_ref[k, 0:5, 0:Y1] = merged.reshape(5, Y1, 128)
            for k in range(2):
                tile = 4 * b + 2 * h + k
                for q in range(5):
                    row = pl.multiple_of((group * 5 + q) * 128, 128)
                    for s in range(3):
                        second_ref[s, tile, pl.ds(row, 128)] = tmp_ref[k, q, s : s + 128].astype(BF16)
        return carry

    lax.fori_loop(0, 4, second_rows, 0)

    def third_rows(b):
        pieces = []
        for tx in range(3):
            for ty in range(3):
                for w in range(3):
                    pieces.append(second_ref[ty, (2 * b + w) % 8, tx * 128 : tx * 128 + 1024])
        rhs = jnp.concatenate([w3_ref[0], w3_ref[1]], axis=1)
        u = leaky(dot(jnp.concatenate(pieces, axis=1), rhs))
        for h in range(2):
            rows_ref[b % 2, h] = u[:, h * 128 : h * 128 + 128]

    def third_planes(b):
        for x in range(8):
            for h in range(2):
                turned = jnp.transpose(rows_ref[b % 2, h, x * 128 : x * 128 + 128], (1, 0))
                for k in range(2):
                    third_ref[2 * h + k, pl.ds(x, 64, stride=8), :] = turned[64 * k : 64 * k + 64]
        for j in range(4):
            out_ref[4 * b + j] = third_ref[j].astype(BF16)
        copy = pltpu.make_async_copy(
            out_ref.at[4 * b : 4 * b + 4], out_any.at[4 * b : 4 * b + 4], out_sem.at[b]
        )
        copy.start()
        return copy

    sent = []
    for b in range(4):
        third_rows(b)
        if b:
            sent.append(third_planes(b - 1))
    sent.append(third_planes(3))
    for copy in sent:
        copy.wait()


def layers(painted, top, bottom, r1, w3, w2):
    whole = pl.BlockSpec(memory_space=pltpu.VMEM)
    anywhere = pl.BlockSpec(memory_space=pl.ANY)
    return pl.pallas_call(
        layers_kernel,
        in_specs=[whole] * 5 + [anywhere],
        out_specs=anywhere,
        out_shape=jax.ShapeDtypeStruct((16, 512, 128), BF16),
        scratch_shapes=[
            VMEM((4, K_TAPS, 128), BF16),
            VMEM((8, 160, 128), F32),
            VMEM((3, 8 * Y1, 128), BF16),
            VMEM((2, 7, 152, 128), F32),
            VMEM((3, 8, 14 * Y1, 128), BF16),
            VMEM((3, 8, 10 * 128, 128), BF16),
            VMEM((2, 2, 1024, 128), F32),
            VMEM((4, 512, 128), F32),
            VMEM((16, 512, 128), BF16),
            pltpu.SemaphoreType.DMA(()),
            pltpu.SemaphoreType.DMA((4,)),
        ],
        compiler_params=pltpu.CompilerParams(vmem_limit_bytes=48 << 20),
        name="layers",
    )(painted, top, bottom, r1, w3, w2)


def twiddle_rows(count):
    position = np.arange(count, dtype=np.int64)
    phase = position[:, None] * position[None, :] % count
    angle = phase.astype(np.float32) * np.float32(2.0 * math.pi / count)
    factor = np.float32(1.0 / math.sqrt(count))
    parts = np.stack([np.cos(angle) * factor, -np.sin(angle) * factor])
    parts = parts.reshape(2 * count, count // 8, 8)
    table = np.zeros((2, 2 * count, count // 8, 2, 8), np.float32)
    for parity in range(2):
        table[parity, :, :, parity, :] = parts
    return table.reshape(4 * count, 2, count).transpose(1, 0, 2)


def transform_kernel(twiddle_ref, in_ref, out_ref):
    lhs = jnp.concatenate([twiddle_ref[0], twiddle_ref[1]], axis=1)
    base = pl.multiple_of(pl.program_id(0) * 256, 256)
    for pair in range(8):
        rhs = jnp.concatenate(
            [
                in_ref[:, pl.ds(base + (2 * pair + k) * 16, 16)].reshape(256, 128)
                for k in range(2)
            ],
            axis=1,
        )
        u = dot(lhs, rhs).astype(BF16)
        for k in range(2):
            for parity in range(2):
                for t in range(2):
                    at = (parity * 2 + t) * 128
                    out_ref[t, 4 * pair + 2 * k + parity, 0] = u[at : at + 128, k * 128 : k * 128 + 128]


def transform(twiddle, moved):
    return pl.pallas_call(
        transform_kernel,
        grid=(2,),
        in_specs=[
            pl.BlockSpec((2, 512, 128), lambda i: (0, 0, 0)),
            pl.BlockSpec(memory_space=pltpu.VMEM),
        ],
        out_specs=pl.BlockSpec((2, 32, 1, 128, 128), lambda i: (0, i, 0, 0, 0)),
        out_shape=jax.ShapeDtypeStruct((2, 64, 1, 128, 128), BF16),
        name="transform",
    )(twiddle, moved)


def in_vmem(value):
    return pltpu.with_memory_space_constraint(value, pltpu.VMEM)


def on_device(particle_values, destination, cell_index, weight_in, weight_mid, weight_out):
    count_x = lax.axis_size("bx")
    count_y = lax.axis_size("by")
    up_y = [(i, (i + 1) % count_y) for i in range(count_y)]
    down_y = [((i + 1) % count_y, i) for i in range(count_y)]

    outgoing = pack(destination.reshape(1, -1), cell_index.reshape(1, -1), particle_values)
    incoming = lax.all_to_all(outgoing, ("bx", "by"), split_axis=0, concat_axis=0, tiled=True)

    r1, w2 = weights(jnp.transpose(weight_in, (0, 3, 1, 2)), weight_mid)
    incoming = in_vmem(incoming)
    painted, first_y, last_y = paint(incoming, r1)
    top = lax.ppermute(last_y, "by", up_y)
    bottom = lax.ppermute(first_y, "by", down_y)
    w3 = late_weights(weight_out)
    third = layers(*(in_vmem(v) for v in (painted, top, bottom, r1, w3)), w2)
    moved = lax.all_to_all(third, "bx", split_axis=0, concat_axis=0, tiled=True)
    twiddle = jnp.asarray(twiddle_rows(count_x * 8), BF16)
    return transform(twiddle, in_vmem(moved))


def solution(mesh):
    placed = (P(None, ("bx", "by")), P(("bx", "by"), None), P(("bx", "by")), P(), P(), P())
    return jax.shard_map(
        on_device,
        mesh=mesh,
        in_specs=placed,
        out_specs=P(None, None, "bx", None, "by"),
        check_vma=False,
    )
```
